32 devices in a mesh: groups: 2 (over x), blk: 16 (over z, y, core).
Axes of the slice: x: 2, y: 2, z: 4, core: 2. Of those that a mesh axis runs over, the one named last changes fastest.
Arguments:
- hidden: bfloat16 [32, 512, 640], P(('groups', 'blk')), parts along dimension 0, may hold values from -6 to 6
- query_weight: bfloat16 [16, 2560, 640], P('blk')
- query_gain: float32 [5120], replicated, may hold values from 0.1 to 32
- frame_cache: bfloat16 [32, 2, 8, 2, 16, 640], P(('groups', 'blk')), parts along dimension 0, may hold values from -8.1 to 8.1
- span_kv: bfloat16 [32, 2, 512, 640], P(('groups', 'blk')), parts along dimension 0, may hold values from -8 to 8
- selected: int32 [4, 12], P('groups'), parts along dimension 0, may hold values from 1 to 13, as said below
- owner: int32 [4, 16], P('groups'), parts along dimension 0, may hold values from 0 to 15, each once within a row
Outputs:
- attended: bfloat16 [32, 512, 640], P(('groups', 'blk')), parts along dimension 0
The draws below stay inside these ranges and needn't reach their ends.
There are 2 independent parts, one for each index of `groups`. The reference program is written for one: setup_inputs(seed, part) draws one part's arguments, and reference() takes and returns one part's arrays. A program takes and returns all parts, laid end to end along the dimension named above; an argument that names none is the same for every part. Nothing has to cross between parts.
Inputs may be any that keep to these rules, and one draw needn't show every extreme that they name: `selected`: each row names 12 different frames strictly between the first frame and the last 2; frame 16 - 3 is always among them. Each row of owner names every device of the part once, so a device keeps one frame of every rollout.
All inputs are finite; a program needn't handle non-finite values.
Results may differ from the reference program's by a relative error of at most 0.012.
The reference program's roundings to bfloat16 on the way count: a program that leaves them out, or rounds other values in their place, can miss the bound.
Values may be sent and summed in bfloat16 or wider, within the bound.
A program may use at most 64 MiB of HBM per device.

```python
import math
import jax
import jax.numpy as jnp
from jax import lax

HEADS = 40
HD = 128
D = 5120
HG = 8
FT = 16
TOK_DEV = 512
GW = 640
ROLLOUTS = 2
RB = 2560
FR = 16
WIN = 2
NSEL = 12
N_BLK = 16


def draw_query_weight(key, part):
    first_key, second_key = jax.random.split(key)
    column = (jnp.arange(N_BLK) % HG)[:, None] * GW + jnp.arange(GW)[None, :]
    rising = 1.0 + 2.0 * column.astype(jnp.float32) / (D - 1)
    spread = jnp.exp(jax.random.uniform(second_key, (D,), minval=0.0, maxval=math.log(10.0)))
    base_values = jax.random.normal(first_key, (N_BLK, RB, GW))
    column_scale = spread[column] * rising
    return (base_values * column_scale[:, None, :] * D ** (-0.5)).astype(jnp.bfloat16)


def draw_query_gain(key, part):
    first_key = jax.random.fold_in(key, 0)
    gains = jnp.exp(jax.random.uniform(first_key, (D,), minval=math.log(0.5), maxval=math.log(2.0)))
    return gains.astype(jnp.float32)


def draw_frame_cache(key, part):
    first_key, second_key = jax.random.split(key)
    full_shape = (N_BLK, ROLLOUTS, HG, 1, FT, GW)
    keys_part = jnp.clip(1.5 * jax.random.normal(first_key, full_shape), -8.0, 8.0)
    values_part = jnp.clip(2.0 * jax.random.normal(second_key, full_shape), -8.0, 8.0)
    return jnp.concatenate([keys_part, values_part], axis=3).astype(jnp.bfloat16)


def draw_selected(key, part):
    middle_count = FR - WIN - 2

    def one_row(row_key):
        order = jax.random.permutation(row_key, middle_count)
        latest = jnp.full((1,), FR - WIN - 1, dtype=jnp.int32)
        return jnp.concatenate([latest, (1 + order[:NSEL - 1]).astype(jnp.int32)])
    return jax.vmap(one_row)(jax.random.split(key, ROLLOUTS))


def levels(own_key, shape, pieces, least, largest):
    factor_of, own = 1.0, jax.random.fold_in(own_key, 6)
    for dim, blocks in pieces:
        draws = jnp.exp(jax.random.uniform(jax.random.fold_in(own, dim), (blocks,), jnp.float32, least / len(pieces), largest / len(pieces)))
        factor_of = factor_of * jnp.repeat(draws, shape[dim] // blocks).reshape([-1 if axis == dim else 1 for axis in range(len(shape))])
    return factor_of


def normal_values(key, extent, width, most, shards=(), kind=jnp.bfloat16):
    values = width * jax.random.normal(key, extent, jnp.float32)
    if shards:
        values = values * levels(key, extent, shards, -0.22, 0.18)
    return jnp.clip(values, -most, most).astype(kind)


def setup_inputs(seed: int = 0, part: int = 0) -> dict:
    arg_keys = jax.random.split(jax.random.key(seed), 8)
    own_keys = jax.random.split(jax.random.fold_in(arg_keys[7], part), 8)
    hidden = normal_values(own_keys[0], (N_BLK, TOK_DEV, GW), 1.0, 6.0, ((0, 16),))
    query_weight = draw_query_weight(jax.random.fold_in(arg_keys[7], 71), part)
    query_gain = draw_query_gain(jax.random.fold_in(arg_keys[7], 71), part)
    frame_cache = draw_frame_cache(jax.random.fold_in(jax.random.fold_in(arg_keys[7], part), 71), part)
    span_kv = normal_values(own_keys[4], (N_BLK, 2, TOK_DEV, GW), 1.5, 8.0, ((0, 16),))
    selected = draw_selected(jax.random.fold_in(jax.random.fold_in(arg_keys[7], part), 71), part)
    owner = jax.vmap(lambda own: jax.random.permutation(own, N_BLK))(jax.random.split(own_keys[6], ROLLOUTS)).reshape((ROLLOUTS, FR)).astype(jnp.int32)
    return {"hidden": hidden, "query_weight": query_weight, "query_gain": query_gain, "frame_cache": frame_cache, "span_kv": span_kv, "selected": selected, "owner": owner}


norm_epsilon = 1e-06

def reference(hidden, query_weight, query_gain, frame_cache, span_kv, selected, owner):
    features = hidden.reshape(ROLLOUTS, HG, TOK_DEV, GW).transpose(0, 2, 1, 3).reshape(ROLLOUTS, TOK_DEV, D)
    weight = query_weight.reshape(ROLLOUTS, HG, RB, GW).transpose(0, 2, 1, 3).reshape(D, D)
    own_pairs = span_kv.reshape(ROLLOUTS, HG, 2, TOK_DEV, GW)
    frame_time = jnp.arange(FR, dtype=jnp.int32)

    def one_slot(inputs):
        slot_features, slot_pairs, rollout = inputs
        query_rows = jnp.dot(slot_features, weight, preferred_element_type=jnp.float32)
        energy = lax.optimization_barrier(jnp.mean(query_rows * query_rows, axis=1, keepdims=True))
        normed = (query_rows * lax.rsqrt(energy + norm_epsilon) * query_gain).astype(jnp.bfloat16)
        frames = frame_cache[owner[rollout], rollout]
        cached = frames.transpose(2, 0, 3, 1, 4).reshape(2, FR * FT, D)
        own_rows = slot_pairs.transpose(1, 2, 0, 3).reshape(2, TOK_DEV, D)
        key_value = jnp.concatenate([cached, own_rows], axis=1)
        chosen = (frame_time == 0) | (frame_time >= FR - WIN) | jnp.any(frame_time[:, None] == selected[rollout][None, :], axis=1)
        visible = jnp.concatenate([jnp.repeat(chosen, FT), jnp.ones((TOK_DEV,), dtype=bool)])
        query_heads = normed.astype(jnp.float32).reshape(TOK_DEV, HEADS, HD)
        key_heads = key_value[0].astype(jnp.float32).reshape(-1, HEADS, HD)
        value_heads = key_value[1].astype(jnp.float32).reshape(-1, HEADS, HD)
        scores = jnp.einsum('qhd,khd->hqk', query_heads, key_heads) * HD ** (-0.5)
        highest = lax.optimization_barrier(jnp.max(jnp.where(visible, scores, -jnp.inf), axis=2, keepdims=True))
        probs = jnp.where(visible, jnp.exp(scores - highest), 0.0)
        totals = lax.optimization_barrier(jnp.sum(probs, axis=2))
        rounded = lax.optimization_barrier(probs.astype(jnp.bfloat16)).astype(jnp.float32)
        mixed_rows = jnp.einsum('hqk,khd->qhd', rounded, value_heads)
        return (mixed_rows / totals.T[:, :, None]).reshape(TOK_DEV, D).astype(jnp.bfloat16)
    outputs = lax.map(one_slot, (features, own_pairs, jnp.arange(ROLLOUTS, dtype=jnp.int32)))
    return outputs.reshape(ROLLOUTS, TOK_DEV, HG, GW).transpose(0, 2, 1, 3).reshape(N_BLK, TOK_DEV, GW)
```

```python
import math

import jax
import jax.numpy as jnp
from jax import lax
from jax.experimental import pallas as pl
from jax.experimental.pallas import tpu as pltpu
from jax.sharding import PartitionSpec as P

HD = 128
HG = 8


norm_epsilon = 1e-06


def from_partner(block, axis, distance):
    count = lax.axis_size(axis)
    route = []
    for low in range(count):
        high = low | 1 << distance
        if high != low and high < count:
            route += [(low, high), (high, low)]
    return lax.ppermute(block, axis, route)


def passed_along(array, axis, by):
    length = lax.axis_size(axis)
    return lax.ppermute(array, axis, [(i, (i + by) % length) for i in range(length)])


def add_columns(running, features, block_piece, offset):
    columns = lax.dynamic_slice_in_dim(features, offset, block_piece.shape[0], 1)
    return running + jnp.dot(columns, block_piece, preferred_element_type=jnp.float32)


def shards(hidden, query_weight, query_gain, frame_cache, span_kv, selected, owner):
    device = lax.axis_index("blk")
    device_count = lax.axis_size("blk")
    slot_count = device_count // HG
    slot_index = device // HG
    group_index = device % HG
    group_width = hidden.shape[2]
    bit_count = HG.bit_length() - 1
    features = hidden[0]
    for bit_number in range(bit_count):
        partner = from_partner(features, "blk", bit_number)
        upper_half = (group_index >> bit_number) % 2 == 1
        features = jnp.where(
            upper_half,
            jnp.concatenate([partner, features], 1),
            jnp.concatenate([features, partner], 1),
        )
    own_block = query_weight[0]
    block_rows = own_block.shape[0]
    running = jnp.zeros((features.shape[0], group_width), jnp.float32)
    half_rows = block_rows // 2
    first_half = own_block[:half_rows]
    second_half = own_block[half_rows:]
    running = add_columns(running, features, first_half, slot_index * block_rows)
    running = add_columns(running, features, second_half, slot_index * block_rows + half_rows)

    def turn_both(turn_index, loop_state):
        partial_sum, leading, trailing = loop_state
        leading = passed_along(leading, "blk", HG)
        trailing = passed_along(trailing, "blk", -HG)
        earlier = (slot_index - turn_index) % slot_count
        later = (slot_index + turn_index) % slot_count
        partial_sum = add_columns(partial_sum, features, leading, earlier * block_rows)
        partial_sum = add_columns(partial_sum, features, trailing, later * block_rows + half_rows)
        return (partial_sum, leading, trailing)

    running, _, _ = lax.fori_loop(1, slot_count, turn_both, (running, first_half, second_half))
    energy = jnp.sum(running * running, axis=1)
    for bit_number in range(bit_count):
        energy = energy + from_partner(energy, "blk", bit_number)
    row_scale = lax.rsqrt(energy / features.shape[1] + norm_epsilon)
    gain_slice = lax.dynamic_slice_in_dim(query_gain, group_index * group_width, group_width)
    query_rows = (running * row_scale[:, None] * gain_slice).astype(jnp.bfloat16)
    outgoing = frame_cache[0]
    outgoing = outgoing.reshape((-1,) + outgoing.shape[2:])
    incoming = lax.all_to_all(outgoing, "blk", split_axis=0, concat_axis=0, tiled=True)
    frame_count = owner.shape[1]
    window_frames = frame_count // 8
    frame_time = jnp.arange(frame_count, dtype=jnp.int32)
    chosen = (
        (frame_time == 0)
        | (frame_time >= frame_count - window_frames)
        | jnp.any(frame_time[:, None] == selected[slot_index][None, :], axis=1)
    )
    placed = owner[slot_index][:, None] == jnp.arange(device_count, dtype=jnp.int32)[None, :]
    owner_kept = jnp.any(placed & chosen[:, None], axis=0)
    frame_tokens = incoming.shape[2]
    key_rows = jnp.concatenate([incoming[:, 0].reshape(-1, group_width), span_kv[0, 0]], 0)
    value_rows = jnp.concatenate([incoming[:, 1].reshape(-1, group_width), span_kv[0, 1]], 0)
    visible = jnp.concatenate(
        [jnp.repeat(owner_kept, frame_tokens), jnp.ones((query_rows.shape[0],), dtype=bool)]
    )
    head_count = group_width // HD

    def one_head(head_index):
        start = head_index * HD
        query_part = lax.dynamic_slice_in_dim(query_rows, start, HD, 1)
        key_part = lax.dynamic_slice_in_dim(key_rows, start, HD, 1)
        value_part = lax.dynamic_slice_in_dim(value_rows, start, HD, 1)
        scores = lax.dot_general(
            query_part, key_part, (((1,), (1,)), ((), ())), preferred_element_type=jnp.float32
        ) * HD ** (-0.5)
        highest = jnp.max(jnp.where(visible, scores, -jnp.inf), axis=1, keepdims=True)
        probs = jnp.where(visible, jnp.exp(scores - highest), 0.0)
        totals = jnp.sum(probs, axis=1, keepdims=True)
        mixed_rows = jnp.dot(
            probs.astype(jnp.bfloat16), value_part, preferred_element_type=jnp.float32
        )
        return (mixed_rows / totals).astype(jnp.bfloat16)

    head_outputs = lax.map(one_head, jnp.arange(head_count, dtype=jnp.int32))
    return jnp.transpose(head_outputs, (1, 0, 2)).reshape(1, query_rows.shape[0], group_width)


CHUNKS = 5
MESH = pl.DeviceIdType.MESH
SPAN_MASKS = ((0, 0), (1, 0), (0, 1), (1, 1))


def flipped(index, y_flip, z_flip):
    if y_flip:
        index = index + 2 - 4 * ((index // 2) % 2)
    if z_flip:
        index = index + 4 - 8 * ((index // 4) % 2)
    return index


def fused_kernel(
    hidden, weight, gain, frames, span, visible, out,
    x_all, w_own, w_far, kv_frames, kv_span, total, energy, scale,
    local_sem, x_send, x_recv, c_send, c_recv, w_send, w_recv, f_send, f_recv,
    k_send, k_recv, e_send, e_recv,
):
    part = lax.axis_index("groups")
    me = lax.axis_index("blk")
    count = 2 * HG
    slot = me // HG
    group = me % HG
    rows = weight.shape[1]
    half = rows // 2
    chunk = half // CHUNKS
    width = hidden.shape[2]
    core_peer = me + 1 - 2 * (me % 2)
    far = (me + HG) % count

    def columns(block):
        return x_all.at[:, pl.ds(pl.multiple_of((block % HG) * width, 128), width)]

    locals_ = [
        pltpu.make_async_copy(hidden.at[0], columns(me), local_sem.at[0]),
        pltpu.make_async_copy(weight.at[0], w_own, local_sem.at[1]),
        pltpu.make_async_copy(span.at[0], kv_span, local_sem.at[2]),
        pltpu.make_async_copy(frames.at[0, slot, group], kv_frames.at[:, me], local_sem.at[3]),
    ]
    for copy in locals_:
        copy.start()

    barrier = pltpu.get_barrier_semaphore()

    def greet(step, carry):
        pl.semaphore_signal(barrier, inc=1, device_id={"blk": (me + step) % count}, device_id_type=MESH)
        return carry

    lax.fori_loop(1, count, greet, 0)
    pl.semaphore_signal(barrier, inc=1, device_id={"groups": 1 - part}, device_id_type=MESH)
    pl.semaphore_wait(barrier, count)

    def far_copy(k, base):
        block = pl.ds(pl.multiple_of(base * half + k * chunk, chunk), chunk)
        return pltpu.make_async_remote_copy(
            weight.at[0, block], w_far.at[block], w_send.at[k], w_recv.at[k],
            device_id={"blk": far}, device_id_type=MESH)

    def side_copy(k, base):
        block = pl.ds(pl.multiple_of(base * half + k * chunk, chunk), chunk)
        return pltpu.make_async_remote_copy(
            w_far.at[block], w_far.at[block], f_send.at[k], f_recv.at[k],
            device_id={"groups": 1 - part}, device_id_type=MESH)

    def span_copy(j):
        return pltpu.make_async_remote_copy(
            hidden.at[0], columns(me), x_send.at[j], x_recv.at[j],
            device_id={"blk": flipped(me, *SPAN_MASKS[j])}, device_id_type=MESH)

    def span_wait(j):
        block = columns(flipped(me, *SPAN_MASKS[j]))
        pltpu.make_async_remote_copy(
            block, block, x_send.at[j], x_recv.at[j],
            device_id={"blk": flipped(me, *SPAN_MASKS[j])}, device_id_type=MESH).wait_recv()

    def core_copy(j, of):
        block = columns(flipped(of, *SPAN_MASKS[j]))
        return pltpu.make_async_remote_copy(
            hidden.at[0] if j == 0 and of is me else block, block, c_send.at[j], c_recv.at[j],
            device_id={"blk": core_peer}, device_id_type=MESH)

    def frame_copy(step):
        to = (me + step) % count
        return pltpu.make_async_remote_copy(
            frames.at[0, to // HG, to % HG], kv_frames.at[:, me], k_send.at[step], k_recv.at[step],
            device_id={"blk": to}, device_id_type=MESH)

    def frame_wait(step):
        come = (me + count - step) % count
        pltpu.make_async_remote_copy(
            kv_frames.at[:, come], kv_frames.at[:, come], k_send.at[step], k_recv.at[step],
            device_id={"blk": come}, device_id_type=MESH).wait_recv()

    def each(start, stop, act):
        def body(i, carry):
            act(i)
            return carry
        lax.fori_loop(start, stop, body, 0)

    for j in (1, 2, 3):
        span_copy(j).start()
    core_copy(0, me).start()
    each(0, CHUNKS, lambda k: far_copy(k, part).start())
    each(1, count, lambda step: frame_copy(step).start())
    for copy in locals_:
        copy.wait()
    for j in (1, 2, 3):
        span_wait(j)
        core_copy(j, me).start()
    for j in range(4):
        core_copy(j, core_peer).wait_recv()

    total[...] = jnp.zeros_like(total)

    def add(w_ref, offset, row):
        at = pl.multiple_of(offset + row, 128)
        total[...] += jnp.dot(
            x_all[:, pl.ds(at, chunk)], w_ref[pl.ds(pl.multiple_of(row, chunk), chunk), :],
            preferred_element_type=jnp.float32)

    each(0, rows // chunk, lambda i: add(w_own, slot * rows, i * chunk))

    def arrive(k):
        far_copy(k, part).wait_recv()
        side_copy(k, part).start()
        add(w_far, (1 - slot) * rows, part * half + k * chunk)
        side_copy(k, 1 - part).wait_recv()
        add(w_far, (1 - slot) * rows, (1 - part) * half + k * chunk)

    each(0, CHUNKS, arrive)

    query = total[...]
    sums = jnp.sum(query * query, axis=1, keepdims=True)
    energy[group] = jnp.transpose(jnp.broadcast_to(sums, (sums.shape[0], 128)))[:8]

    def energy_copy(step):
        to = (group + step) % HG
        return pltpu.make_async_remote_copy(
            energy.at[group], energy.at[group], e_send.at[step], e_recv.at[step],
            device_id={"blk": slot * HG + to}, device_id_type=MESH)

    def energy_wait(step):
        come = (group + HG - step) % HG
        pltpu.make_async_remote_copy(
            energy.at[come], energy.at[come], e_send.at[step], e_recv.at[step],
            device_id={"blk": slot * HG + come}, device_id_type=MESH).wait_recv()

    each(1, HG, lambda step: energy_copy(step).start())
    each(1, count, frame_wait)
    each(1, HG, energy_wait)
    mean = jnp.sum(energy[...], axis=0) / (HG * width)
    row_scale = lax.rsqrt(mean + norm_epsilon)
    scale[...] = jnp.transpose(jnp.concatenate([row_scale] * 16, axis=0))

    shown = visible[...] > 0.5
    factor = HD ** (-0.5) * math.log2(math.e)
    contract = (((1,), (1,)), ((), ()))

    def one_head(h):
        at = pl.ds(pl.multiple_of(h * HD, HD), HD)
        query_part = (total[:, at] * scale[...] * gain[:, at]).astype(jnp.bfloat16)
        key_old = kv_frames[0, :, :, at].reshape(-1, HD)
        value_old = kv_frames[1, :, :, at].reshape(-1, HD)
        key_new = kv_span[0, :, at]
        value_new = kv_span[1, :, at]
        old = lax.dot_general(query_part, key_old, contract, preferred_element_type=jnp.float32)
        new = lax.dot_general(query_part, key_new, contract, preferred_element_type=jnp.float32)
        old = jnp.where(shown, old, -jnp.inf)
        highest = jnp.maximum(
            jnp.max(old, axis=1, keepdims=True), jnp.max(new, axis=1, keepdims=True))
        old = jnp.exp2((old - highest) * factor)
        new = jnp.exp2((new - highest) * factor)
        totals = jnp.sum(old, axis=1, keepdims=True) + jnp.sum(new, axis=1, keepdims=True)
        mixed = jnp.dot(old.astype(jnp.bfloat16), value_old, preferred_element_type=jnp.float32)
        mixed += jnp.dot(new.astype(jnp.bfloat16), value_new, preferred_element_type=jnp.float32)
        out[0, :, at] = (mixed / totals).astype(jnp.bfloat16)

    each(0, width // HD, one_head)

    for j in (1, 2, 3):
        span_copy(j).wait_send()
    for j in range(4):
        core_copy(j, me).wait_send()
    each(0, CHUNKS, lambda k: far_copy(k, part).wait_send())
    each(0, CHUNKS, lambda k: side_copy(k, part).wait_send())
    each(1, count, lambda step: frame_copy(step).wait_send())
    each(1, HG, lambda step: energy_copy(step).wait_send())


def fused(hidden, query_weight, query_gain, frame_cache, span_kv, selected, owner):
    device = lax.axis_index("blk")
    device_count = lax.axis_size("blk")
    slot_index = device // HG
    group_index = device % HG
    tokens, width = hidden.shape[1:]
    rows = query_weight.shape[1]
    frame_tokens = frame_cache.shape[4]
    frame_count = owner.shape[1]
    window_frames = frame_count // 8
    frame_time = jnp.arange(frame_count, dtype=jnp.int32)
    chosen = (
        (frame_time == 0)
        | (frame_time >= frame_count - window_frames)
        | jnp.any(frame_time[:, None] == selected[slot_index][None, :], axis=1)
    )
    placed = owner[slot_index][:, None] == jnp.arange(device_count, dtype=jnp.int32)[None, :]
    owner_kept = jnp.any(placed & chosen[:, None], axis=0)
    visible = jnp.repeat(owner_kept, frame_tokens).astype(jnp.float32)[None, :]
    gain_slice = lax.dynamic_slice_in_dim(query_gain, group_index * width, width)[None, :]
    dma = pltpu.SemaphoreType.DMA
    anywhere = pl.BlockSpec(memory_space=pl.ANY)
    inside = pl.BlockSpec(memory_space=pltpu.VMEM)
    bf16, f32 = jnp.bfloat16, jnp.float32
    return pl.pallas_call(
        fused_kernel,
        out_shape=jax.ShapeDtypeStruct((1, tokens, width), bf16),
        in_specs=[anywhere, anywhere, inside, anywhere, anywhere, inside],
        out_specs=inside,
        scratch_shapes=[
            pltpu.VMEM((tokens, HG * width), bf16),
            pltpu.VMEM((rows, width), bf16),
            pltpu.VMEM((rows, width), bf16),
            pltpu.VMEM((2, device_count, frame_tokens, width), bf16),
            pltpu.VMEM((2, tokens, width), bf16),
            pltpu.VMEM((tokens, width), f32),
            pltpu.VMEM((HG, 8, tokens), f32),
            pltpu.VMEM((tokens, 128), f32),
            dma((4,)), dma((4,)), dma((4,)), dma((4,)), dma((4,)),
            dma((CHUNKS,)), dma((CHUNKS,)), dma((CHUNKS,)), dma((CHUNKS,)),
            dma((device_count,)), dma((device_count,)), dma((HG,)), dma((HG,)),
        ],
        compiler_params=pltpu.CompilerParams(
            collective_id=0, has_side_effects=True, vmem_limit_bytes=48 * 1024 * 1024),
    )(hidden, query_weight, gain_slice, frame_cache, span_kv, visible)


def solution(mesh):
    small = mesh.shape["blk"] == 2 * HG and mesh.shape["groups"] == 2
    body = fused if small else shards
    in_specs = (
        P(("groups", "blk"), None, None),
        P("blk", None, None),
        P(),
        P(("groups", "blk"), None, None, None, None, None),
        P(("groups", "blk"), None, None, None),
        P("groups", None),
        P("groups", None),
    )
    out_specs = P(("groups", "blk"), None, None)
    return jax.shard_map(body, mesh=mesh, in_specs=in_specs, out_specs=out_specs, check_vma=False)
```

```python
import math

import jax
import jax.numpy as jnp
from jax import lax
from jax.experimental import pallas as pl
from jax.experimental.pallas import tpu as pltpu
from jax.sharding import PartitionSpec as P

HD = 128
HG = 8


norm_epsilon = 1e-06


def from_partner(block, axis, distance):
    count = lax.axis_size(axis)
    route = []
    for low in range(count):
        high = low | 1 << distance
        if high != low and high < count:
            route += [(low, high), (high, low)]
    return lax.ppermute(block, axis, route)


def passed_along(array, axis, by):
    length = lax.axis_size(axis)
    return lax.ppermute(array, axis, [(i, (i + by) % length) for i in range(length)])


def add_columns(running, features, block_piece, offset):
    columns = lax.dynamic_slice_in_dim(features, offset, block_piece.shape[0], 1)
    return running + jnp.dot(columns, block_piece, preferred_element_type=jnp.float32)


def shards(hidden, query_weight, query_gain, frame_cache, span_kv, selected, owner):
    device = lax.axis_index("blk")
    device_count = lax.axis_size("blk")
    slot_count = device_count // HG
    slot_index = device // HG
    group_index = device % HG
    group_width = hidden.shape[2]
    bit_count = HG.bit_length() - 1
    features = hidden[0]
    for bit_number in range(bit_count):
        partner = from_partner(features, "blk", bit_number)
        upper_half = (group_index >> bit_number) % 2 == 1
        features = jnp.where(
            upper_half,
            jnp.concatenate([partner, features], 1),
            jnp.concatenate([features, partner], 1),
        )
    own_block = query_weight[0]
    block_rows = own_block.shape[0]
    running = jnp.zeros((features.shape[0], group_width), jnp.float32)
    half_rows = block_rows // 2
    first_half = own_block[:half_rows]
    second_half = own_block[half_rows:]
    running = add_columns(running, features, first_half, slot_index * block_rows)
    running = add_columns(running, features, second_half, slot_index * block_rows + half_rows)

    def turn_both(turn_index, loop_state):
        partial_sum, leading, trailing = loop_state
        leading = passed_along(leading, "blk", HG)
        trailing = passed_along(trailing, "blk", -HG)
        earlier = (slot_index - turn_index) % slot_count
        later = (slot_index + turn_index) % slot_count
        partial_sum = add_columns(partial_sum, features, leading, earlier * block_rows)
        partial_sum = add_columns(partial_sum, features, trailing, later * block_rows + half_rows)
        return (partial_sum, leading, trailing)

    running, _, _ = lax.fori_loop(1, slot_count, turn_both, (running, first_half, second_half))
    energy = jnp.sum(running * running, axis=1)
    for bit_number in range(bit_count):
        energy = energy + from_partner(energy, "blk", bit_number)
    row_scale = lax.rsqrt(energy / features.shape[1] + norm_epsilon)
    gain_slice = lax.dynamic_slice_in_dim(query_gain, group_index * group_width, group_width)
    query_rows = (running * row_scale[:, None] * gain_slice).astype(jnp.bfloat16)
    outgoing = frame_cache[0]
    outgoing = outgoing.reshape((-1,) + outgoing.shape[2:])
    incoming = lax.all_to_all(outgoing, "blk", split_axis=0, concat_axis=0, tiled=True)
    frame_count = owner.shape[1]
    window_frames = frame_count // 8
    frame_time = jnp.arange(frame_count, dtype=jnp.int32)
    chosen = (
        (frame_time == 0)
        | (frame_time >= frame_count - window_frames)
        | jnp.any(frame_time[:, None] == selected[slot_index][None, :], axis=1)
    )
    placed = owner[slot_index][:, None] == jnp.arange(device_count, dtype=jnp.int32)[None, :]
    owner_kept = jnp.any(placed & chosen[:, None], axis=0)
    frame_tokens = incoming.shape[2]
    key_rows = jnp.concatenate([incoming[:, 0].reshape(-1, group_width), span_kv[0, 0]], 0)
    value_rows = jnp.concatenate([incoming[:, 1].reshape(-1, group_width), span_kv[0, 1]], 0)
    visible = jnp.concatenate(
        [jnp.repeat(owner_kept, frame_tokens), jnp.ones((query_rows.shape[0],), dtype=bool)]
    )
    head_count = group_width // HD

    def one_head(head_index):
        start = head_index * HD
        query_part = lax.dynamic_slice_in_dim(query_rows, start, HD, 1)
        key_part = lax.dynamic_slice_in_dim(key_rows, start, HD, 1)
        value_part = lax.dynamic_slice_in_dim(value_rows, start, HD, 1)
        scores = lax.dot_general(
            query_part, key_part, (((1,), (1,)), ((), ())), preferred_element_type=jnp.float32
        ) * HD ** (-0.5)
        highest = jnp.max(jnp.where(visible, scores, -jnp.inf), axis=1, keepdims=True)
        probs = jnp.where(visible, jnp.exp(scores - highest), 0.0)
        totals = jnp.sum(probs, axis=1, keepdims=True)
        mixed_rows = jnp.dot(
            probs.astype(jnp.bfloat16), value_part, preferred_element_type=jnp.float32
        )
        return (mixed_rows / totals).astype(jnp.bfloat16)

    head_outputs = lax.map(one_head, jnp.arange(head_count, dtype=jnp.int32))
    return jnp.transpose(head_outputs, (1, 0, 2)).reshape(1, query_rows.shape[0], group_width)


CHUNKS = 10
AHEAD = 3
EARLY = 3
MESH = pl.DeviceIdType.MESH
SPAN_MASKS = ((0, 0), (1, 0), (0, 1), (1, 1))


def flipped(index, y_flip, z_flip):
    if y_flip:
        index = index + 2 - 4 * ((index // 2) % 2)
    if z_flip:
        index = index + 4 - 8 * ((index // 4) % 2)
    return index


def fused_kernel(
    hidden, weight, gain, frames, span, visible, out,
    x_all, w_own, w_far, kv_frames, kv_span, total, energy, scale,
    local_sem, x_send, x_recv, c_send, c_recv, w_send, w_recv, f_send, f_recv,
    k_send, k_recv, e_send, e_recv,
):
    part = lax.axis_index("groups")
    me = lax.axis_index("blk")
    count = 2 * HG
    slot = me // HG
    group = me % HG
    rows = weight.shape[1]
    half = rows // 2
    chunk = half // CHUNKS
    width = hidden.shape[2]
    core_peer = me + 1 - 2 * (me % 2)
    far = (me + HG) % count

    def columns(block):
        return x_all.at[:, pl.ds(pl.multiple_of((block % HG) * width, 128), width)]

    locals_ = [
        pltpu.make_async_copy(hidden.at[0], columns(me), local_sem.at[0]),
        pltpu.make_async_copy(weight.at[0], w_own, local_sem.at[1]),
        pltpu.make_async_copy(span.at[0], kv_span, local_sem.at[2]),
        pltpu.make_async_copy(frames.at[0, slot, group], kv_frames.at[:, me], local_sem.at[3]),
    ]
    for copy in locals_:
        copy.start()

    barrier = pltpu.get_barrier_semaphore()

    def greet(step, carry):
        pl.semaphore_signal(barrier, inc=1, device_id={"blk": (me + step) % count}, device_id_type=MESH)
        return carry

    lax.fori_loop(1, count, greet, 0)
    pl.semaphore_signal(barrier, inc=1, device_id={"groups": 1 - part}, device_id_type=MESH)
    pl.semaphore_wait(barrier, count)

    def far_copy(k, base):
        block = pl.ds(pl.multiple_of(base * half + k * chunk, chunk), chunk)
        return pltpu.make_async_remote_copy(
            weight.at[0, block], w_far.at[block], w_send.at[k], w_recv.at[k],
            device_id={"blk": far}, device_id_type=MESH)

    def side_copy(k, base):
        block = pl.ds(pl.multiple_of(base * half + k * chunk, chunk), chunk)
        return pltpu.make_async_remote_copy(
            w_far.at[block], w_far.at[block], f_send.at[k], f_recv.at[k],
            device_id={"groups": 1 - part}, device_id_type=MESH)

    def span_copy(j):
        return pltpu.make_async_remote_copy(
            hidden.at[0], columns(me), x_send.at[j], x_recv.at[j],
            device_id={"blk": flipped(me, *SPAN_MASKS[j])}, device_id_type=MESH)

    def span_wait(j):
        block = columns(flipped(me, *SPAN_MASKS[j]))
        pltpu.make_async_remote_copy(
            block, block, x_send.at[j], x_recv.at[j],
            device_id={"blk": flipped(me, *SPAN_MASKS[j])}, device_id_type=MESH).wait_recv()

    def core_copy(j, of):
        block = columns(flipped(of, *SPAN_MASKS[j]))
        return pltpu.make_async_remote_copy(
            hidden.at[0] if j == 0 and of is me else block, block, c_send.at[j], c_recv.at[j],
            device_id={"blk": core_peer}, device_id_type=MESH)

    def frame_copy(step):
        to = (me + step) % count
        return pltpu.make_async_remote_copy(
            frames.at[0, to // HG, to % HG], kv_frames.at[:, me], k_send.at[step], k_recv.at[step],
            device_id={"blk": to}, device_id_type=MESH)

    def frame_wait(step):
        come = (me + count - step) % count
        pltpu.make_async_remote_copy(
            kv_frames.at[:, come], kv_frames.at[:, come], k_send.at[step], k_recv.at[step],
            device_id={"blk": come}, device_id_type=MESH).wait_recv()

    def each(start, stop, act):
        def body(i, carry):
            act(i)
            return carry
        lax.fori_loop(start, stop, body, 0)

    for j in (1, 2, 3):
        span_copy(j).start()
    core_copy(0, me).start()
    each(0, AHEAD, lambda k: far_copy(k, part).start())
    for copy in locals_:
        copy.wait()

    def hand_on(k):
        far_copy(k, part).wait_recv()
        side_copy(k, part).start()
        far_copy(k, part).wait_send()

        @pl.when(k < CHUNKS - AHEAD)
        def _():
            far_copy(k + AHEAD, part).start()

        @pl.when(k == CHUNKS - AHEAD)
        def _():
            each(1, count, lambda step: frame_copy(step).start())

    each(0, EARLY, hand_on)
    for j in (1, 2, 3):
        span_wait(j)
        core_copy(j, me).start()
    for j in range(4):
        core_copy(j, core_peer).wait_recv()

    total[...] = jnp.zeros_like(total)

    def add(w_ref, offset, row, depth):
        at = pl.multiple_of(offset + row, 128)
        total[...] += jnp.dot(
            x_all[:, pl.ds(at, depth)], w_ref[pl.ds(pl.multiple_of(row, depth), depth), :],
            preferred_element_type=jnp.float32)

    def add_far(k):
        add(w_far, (1 - slot) * rows, part * half + k * chunk, chunk)

    def add_side(k):
        side_copy(k, 1 - part).wait_recv()
        add(w_far, (1 - slot) * rows, (1 - part) * half + k * chunk, chunk)

    def arrive(k):
        hand_on(k)
        first = 2 * (k - EARLY)

        @pl.when(first < rows // (2 * chunk))
        def _():
            for i in (first, first + 1):
                add(w_own, slot * rows, i * 2 * chunk, 2 * chunk)

        add_far(k - EARLY)
        add_side(k - EARLY)

    each(EARLY, CHUNKS, arrive)

    def finish(k):
        add_far(k)
        add_side(k)

    each(CHUNKS - EARLY, CHUNKS, finish)

    query = total[...]
    sums = jnp.sum(query * query, axis=1, keepdims=True)
    energy[group] = jnp.transpose(jnp.broadcast_to(sums, (sums.shape[0], 128)))[:8]

    def energy_copy(step):
        to = (group + step) % HG
        return pltpu.make_async_remote_copy(
            energy.at[group], energy.at[group], e_send.at[step], e_recv.at[step],
            device_id={"blk": slot * HG + to}, device_id_type=MESH)

    def energy_wait(step):
        come = (group + HG - step) % HG
        pltpu.make_async_remote_copy(
            energy.at[come], energy.at[come], e_send.at[step], e_recv.at[step],
            device_id={"blk": slot * HG + come}, device_id_type=MESH).wait_recv()

    each(1, HG, lambda step: energy_copy(step).start())
    each(1, HG, energy_wait)
    mean = jnp.sum(energy[...], axis=0) / (HG * width)
    row_scale = lax.rsqrt(mean + norm_epsilon)
    scale[...] = jnp.transpose(jnp.concatenate([row_scale] * 16, axis=0))

    each(1, count, frame_wait)
    shown = visible[...] > 0.5
    factor = HD ** (-0.5) * math.log2(math.e)
    contract = (((1,), (1,)), ((), ()))

    def one_head(h):
        at = pl.ds(pl.multiple_of(h * HD, HD), HD)
        query_part = (total[:, at] * scale[...] * gain[:, at]).astype(jnp.bfloat16)
        key_old = kv_frames[0, :, :, at].reshape(-1, HD)
        value_old = kv_frames[1, :, :, at].reshape(-1, HD)
        key_new = kv_span[0, :, at]
        value_new = kv_span[1, :, at]
        old = lax.dot_general(query_part, key_old, contract, preferred_element_type=jnp.float32)
        new = lax.dot_general(query_part, key_new, contract, preferred_element_type=jnp.float32)
        old = jnp.where(shown, old, -jnp.inf)
        highest = jnp.maximum(
            jnp.max(old, axis=1, keepdims=True), jnp.max(new, axis=1, keepdims=True))
        old = jnp.exp2((old - highest) * factor)
        new = jnp.exp2((new - highest) * factor)
        totals = jnp.sum(old, axis=1, keepdims=True) + jnp.sum(new, axis=1, keepdims=True)
        mixed = jnp.dot(old.astype(jnp.bfloat16), value_old, preferred_element_type=jnp.float32)
        mixed += jnp.dot(new.astype(jnp.bfloat16), value_new, preferred_element_type=jnp.float32)
        out[0, :, at] = (mixed / totals).astype(jnp.bfloat16)

    each(0, width // HD, one_head)

    for j in (1, 2, 3):
        span_copy(j).wait_send()
    for j in range(4):
        core_copy(j, me).wait_send()
    each(0, CHUNKS, lambda k: side_copy(k, part).wait_send())
    each(1, count, lambda step: frame_copy(step).wait_send())
    each(1, HG, lambda step: energy_copy(step).wait_send())


def fused(hidden, query_weight, query_gain, frame_cache, span_kv, selected, owner):
    device = lax.axis_index("blk")
    device_count = lax.axis_size("blk")
    slot_index = device // HG
    group_index = device % HG
    tokens, width = hidden.shape[1:]
    rows = query_weight.shape[1]
    frame_tokens = frame_cache.shape[4]
    frame_count = owner.shape[1]
    window_frames = frame_count // 8
    frame_time = jnp.arange(frame_count, dtype=jnp.int32)
    chosen = (
        (frame_time == 0)
        | (frame_time >= frame_count - window_frames)
        | jnp.any(frame_time[:, None] == selected[slot_index][None, :], axis=1)
    )
    placed = owner[slot_index][:, None] == jnp.arange(device_count, dtype=jnp.int32)[None, :]
    owner_kept = jnp.any(placed & chosen[:, None], axis=0)
    visible = jnp.repeat(owner_kept, frame_tokens).astype(jnp.float32)[None, :]
    gain_slice = lax.dynamic_slice_in_dim(query_gain, group_index * width, width)[None, :]
    dma = pltpu.SemaphoreType.DMA
    anywhere = pl.BlockSpec(memory_space=pltpu.HBM)
    inside = pl.BlockSpec(memory_space=pltpu.VMEM)
    bf16, f32 = jnp.bfloat16, jnp.float32
    return pl.pallas_call(
        fused_kernel,
        out_shape=jax.ShapeDtypeStruct((1, tokens, width), bf16),
        in_specs=[anywhere, anywhere, inside, anywhere, anywhere, inside],
        out_specs=inside,
        scratch_shapes=[
            pltpu.VMEM((tokens, HG * width), bf16),
            pltpu.VMEM((rows, width), bf16),
            pltpu.VMEM((rows, width), bf16),
            pltpu.VMEM((2, device_count, frame_tokens, width), bf16),
            pltpu.VMEM((2, tokens, width), bf16),
            pltpu.VMEM((tokens, width), f32),
            pltpu.VMEM((HG, 8, tokens), f32),
            pltpu.VMEM((tokens, 128), f32),
            dma((4,)), dma((4,)), dma((4,)), dma((4,)), dma((4,)),
            dma((CHUNKS,)), dma((CHUNKS,)), dma((CHUNKS,)), dma((CHUNKS,)),
            dma((device_count,)), dma((device_count,)), dma((HG,)), dma((HG,)),
        ],
        compiler_params=pltpu.CompilerParams(
            collective_id=0, has_side_effects=True, vmem_limit_bytes=48 * 1024 * 1024),
    )(hidden, query_weight, gain_slice, frame_cache, span_kv, visible)


def solution(mesh):
    small = mesh.shape["blk"] == 2 * HG and mesh.shape["groups"] == 2
    body = fused if small else shards
    in_specs = (
        P(("groups", "blk"), None, None),
        P("blk", None, None),
        P(),
        P(("groups", "blk"), None, None, None, None, None),
        P(("groups", "blk"), None, None, None),
        P("groups", None),
        P("groups", None),
    )
    out_specs = P(("groups", "blk"), None, None)
    return jax.shard_map(body, mesh=mesh, in_specs=in_specs, out_specs=out_specs, check_vma=False)
```
